256 devices in a mesh: shot: 16 (over x_lo, z), rcv: 8 (over y, x_hi), surf: 2 (over core).
Axes of the slice: x: 4 (x_hi: 2, x_lo: 2; x = x_hi * 2 + x_lo), y: 4, z: 8, core: 2. Of those that a mesh axis runs over, the one named last changes fastest.
Arguments:
- traces: bfloat16 [2, 16384, 256], P('surf', 'shot'), may hold values from -6 to 6
- trace_block: int32 [2, 16384, 1], P('surf', 'shot'), may hold values from 0 to 15; in each aligned block of 128 rows (0 to 127, 128 to 255, ..., all dimensions but the last counted through in order) at most 16 rows name the same one
- trace_shot: int32 [2, 16384], P('surf', 'shot'), may hold values from 0 to 15
- trace_point: int32 [2, 16384], P('surf', 'shot'), may hold values from 0 to 255
- recv_panel: bfloat16 [129, 2, 512, 1024], P(None, None, ('shot', 'surf'), 'rcv'), may hold values from -0.375 to 0.375
Outputs:
- multiples: bfloat16 [129, 2, 256, 1024], P(None, None, ('shot', 'surf'), 'rcv')
The draws below stay inside these ranges and needn't reach their ends.
Inputs may be any that keep to these rules, and one draw needn't show every extreme that they name: `trace_block`: in each aligned block of 128 rows, at most 16 rows name one shot block.
All inputs are finite; a program needn't handle non-finite values.
Results may differ from the reference program's by a relative error of at most 0.012.
Values may be sent and summed in bfloat16 or wider, within the bound.
A program may use at most 64 MiB of HBM per device.

```python
import math
import jax
import jax.numpy as jnp
import numpy as np
from jax import lax

WINDOW = 256
F = 129
K = 512
SHOTS_PER_INDEX = 16
RC_DEV = 128
TR_DEV = 1024
PART_ROWS = 128
CAP = 16
KD = 256
RCVS = 1024
N_SHOT = 16
N_RCV = 8
N_SURF = 2


def plant(entries, own_key, smallest, top_value):
    longest = entries.shape.index(max(entries.shape))
    spots = []
    for shift in (0, 1):
        where = [jax.random.randint(jax.random.fold_in(own_key, axis), (), 0, length) for axis, length in enumerate(entries.shape)]
        where[longest] = (where[longest] + shift) % entries.shape[longest]
        spots.append(tuple(where))
    return entries.at[spots[0]].set(smallest).at[spots[1]].set(top_value)


def levels(key, extent, pieces, low, largest):
    gain = 1.0
    for dim, parts in pieces:
        draws = jax.random.uniform(jax.random.fold_in(jax.random.fold_in(key, 6), dim), (parts,), jnp.float32, low / len(pieces), largest / len(pieces))
        gain = gain * jnp.repeat(jnp.exp(draws), extent[dim] // parts).reshape((-1,) + (1,) * (len(extent) - 1 - dim))
    return gain


def deal_out(key, own, number, rows, amount, top, reach, lean):
    sequence = jax.random.permutation(key, amount)
    heavy_load, usual = shares(amount, rows * top, reach, lean, True), shares(amount, rows * top, reach, lean, False)
    places = jnp.arange(amount)

    def named(sizes, offset_by):
        used = int((sizes > 0).sum())
        fixed = max(1, used // 4)
        moved = fixed + (places - fixed + offset_by * (used - fixed)) % max(1, amount - fixed)
        return jnp.zeros((amount,), jnp.int32).at[sequence[jnp.where(places < fixed, places, moved)]].set(jnp.asarray(sizes, jnp.int32))

    sizes = jnp.where(number % 4 == 0, named(heavy_load, number // 4), named(usual, number - number // 4 - 1))
    mixed = jax.random.permutation(jax.random.fold_in(own, 3), amount)
    giver, taker = mixed[0:amount // 2 * 2:2], mixed[1:amount // 2 * 2:2]
    margin = jnp.minimum(sizes[giver] - 1, reach - sizes[taker]) // 2
    margin = jnp.where((giver == sequence[0]) | (taker == sequence[0]) | (sizes[taker] == 0), 0, jnp.maximum(margin, 0))
    moved = jax.random.randint(jax.random.fold_in(own, 4), (amount // 2,), 0, 1 << 20) % (margin + 1)
    sizes = sizes.at[giver].add(-moved).at[taker].add(moved)
    labels = jnp.searchsorted(jnp.cumsum(sizes), jnp.arange(rows * top), side="right").astype(jnp.int32)
    table = labels.reshape(top, rows).T
    table = table[jax.random.permutation(jax.random.fold_in(own, 1), rows)]
    offset_by = jax.random.randint(jax.random.fold_in(own, 2), (rows, 1), 0, top)
    return jnp.take_along_axis(table, (jnp.arange(top)[None, :] + offset_by) % top, axis=1)


def shares(amount, total, limit, skew, full):
    weights = [(1 << 20) // math.isqrt(standing ** skew) + 1 for standing in range(1, amount + 1)]
    largest = limit if full else min(limit, max(-(-total // amount), total * weights[0] // sum(weights)))
    least = 1 if total - largest >= amount - 1 else 0
    given, rest = [largest] + [least] * (amount - 1), total - largest - least * (amount - 1)
    while rest > 0:
        candidates = [i for i in range(1, amount) if given[i] < largest] or [i for i in range(1, amount) if given[i] < limit]
        pool, remaining = sum([weights[i] for i in candidates]), rest
        for i in candidates:
            more = min(limit - given[i], max(1, remaining * weights[i] // pool), rest)
            given[i] = given[i] + more
            rest = rest - more
    return np.array(given)


def gaussian(own_key, shape, deviation, bound, pieces=(), held_as=jnp.bfloat16):
    entries = deviation * jax.random.normal(own_key, shape, jnp.float32)
    if pieces:
        entries = entries * levels(own_key, shape, pieces, -0.22, 0.18)
    return jnp.clip(entries, -bound, bound).astype(held_as)


def setup_inputs(seed: int = 0) -> dict:
    key_list = jax.random.split(jax.random.key(seed), 6)
    traces = gaussian(key_list[0], (N_SURF, TR_DEV * N_SHOT, WINDOW), 1.0, 6.0, ((0, 2), (1, 16)))
    trace_block_keys = jax.random.split(jax.random.fold_in(key_list[1], 1), N_SURF * (TR_DEV * N_SHOT) // PART_ROWS)
    trace_block_turns = jax.random.permutation(jax.random.fold_in(key_list[1], 3), N_SURF * (TR_DEV * N_SHOT) // PART_ROWS)
    trace_block = jax.vmap(lambda own, number: deal_out(jax.random.fold_in(key_list[1], 2), own, number, PART_ROWS, N_SHOT, 1, CAP, 2))(trace_block_keys, trace_block_turns).reshape((N_SURF, TR_DEV * N_SHOT, 1))
    trace_shot = plant(jax.random.randint(key_list[2], (N_SURF, TR_DEV * N_SHOT), 0, SHOTS_PER_INDEX), jax.random.fold_in(key_list[2], 1), 0, SHOTS_PER_INDEX - 1).astype(jnp.int32)
    trace_point = plant(jax.random.randint(key_list[3], (N_SURF, TR_DEV * N_SHOT), 0, KD), jax.random.fold_in(key_list[3], 1), 0, KD - 1).astype(jnp.int32)
    recv_panel = gaussian(key_list[4], (F, 2, K, RCVS), (K // 2) ** -0.5, 0.375, ((2, 32), (3, 8)))
    return {"traces": traces, "trace_block": trace_block, "trace_shot": trace_shot, "trace_point": trace_point, "recv_panel": recv_panel}


def rounded(values):
    return lax.optimization_barrier(values.astype(jnp.bfloat16)).astype(jnp.float32)


def reference(traces, trace_block, trace_shot, trace_point, recv_panel):
    half_window_width = K // N_SURF
    block_width = K // (N_SHOT * N_SURF)
    shot_total = SHOTS_PER_INDEX * N_SHOT
    rcv_total = RC_DEV * N_RCV
    samples = traces.astype(jnp.float32)
    spectrum = jnp.fft.rfft(samples, axis=-1) * (WINDOW ** -0.5)
    pairs = rounded(jnp.stack([jnp.real(spectrum), jnp.imag(spectrum)], axis=2))
    half_index = lax.broadcasted_iota(jnp.int32, trace_shot.shape, 0)
    source_shot_index = trace_block[:, :, 0] * SHOTS_PER_INDEX + trace_shot
    bin_position_index = ((source_shot_index * N_SURF + half_index) * half_window_width + trace_point).reshape(-1).astype(jnp.int32)
    flat_rows = pairs.reshape(-1, 2, F)
    sums = jax.ops.segment_sum(flat_rows, bin_position_index, num_segments=shot_total * K)
    coverage = jax.ops.segment_sum(jnp.ones(bin_position_index.shape, jnp.float32), bin_position_index, num_segments=shot_total * K)
    panel = (sums / jnp.maximum(coverage, 1.0)[:, None, None]).astype(jnp.bfloat16)
    panel = panel.reshape(shot_total, N_SURF, half_window_width, 2, F).transpose(4, 1, 3, 0, 2)
    receiver = recv_panel.reshape(F, 2, N_SHOT, N_SURF, block_width, rcv_total)
    receiver = receiver.transpose(0, 3, 1, 2, 4, 5).reshape(F, N_SURF, 2, half_window_width, rcv_total)

    def one_freq(pair):
        left_edge = pair[0].astype(jnp.float32)
        right_edge = pair[1].astype(jnp.float32)

        def product(first, second):
            return jnp.einsum("hsk,hkr->hsr", first, second)

        real_part = product(left_edge[:, 0], right_edge[:, 0]) - product(left_edge[:, 1], right_edge[:, 1])
        imag_part = product(left_edge[:, 0], right_edge[:, 1]) + product(left_edge[:, 1], right_edge[:, 0])
        partial_value = rounded(jnp.stack([real_part, imag_part], axis=1))
        return jnp.sum(partial_value, axis=0).astype(jnp.bfloat16)

    return lax.map(one_freq, (panel, receiver))
```

```python
import math

import jax
import jax.numpy as jnp
import numpy as np
from jax import lax
from jax.experimental import pallas as pl
from jax.experimental.pallas import tpu as pltpu
from jax.sharding import PartitionSpec as P

SHOTS = 16
SPAN = 8
PART = 128
PARTS = 8
CAP = 16
POINTS = 256
RCV = 128
F32 = jnp.float32
BF16 = jnp.bfloat16
NT = (((1,), (1,)), ((), ()))


def transform_table(window, freqs):
    phase = (np.arange(freqs)[:, None] * np.arange(window)[None, :] % window) * (2 * math.pi / window)
    table = np.zeros((2 * freqs + 6, window), np.float32)
    table[0 : 2 * freqs : 2] = np.cos(phase) / math.sqrt(window)
    table[1 : 2 * freqs : 2] = -np.sin(phase) / math.sqrt(window)
    high = table.astype(BF16)
    return high, (table - high.astype(np.float32)).astype(BF16)


def kernel(
    traces, block_ids, shot_ids, point_ids, table_high, table_low, recv, out,
    spec_out, spec_in, last_out, last_in, meta_out, meta_in, slots, extras, panel,
    points, part, other, final,
    spec_send, spec_recv, last_send, last_recv, meta_send, meta_recv,
    recv_send, recv_recv, swap_send, swap_recv, out_send, out_recv,
):
    me = lax.axis_index("shot")
    core = lax.axis_index("surf")
    column, ring = me // 8, me % 8

    def ahead(step):
        return (column + step % 2) % 2 * 8 + (ring + step // 2) % 8

    def behind(step):
        return (column + step % 2) % 2 * 8 + (ring + 8 - step // 2) % 8

    def remote(src, dst, send, arrive, **where):
        return pltpu.make_async_remote_copy(
            src_ref=src, dst_ref=dst, send_sem=send, recv_sem=arrive,
            device_id=where, device_id_type=pl.DeviceIdType.MESH,
        )

    last_in[...] = jnp.zeros_like(last_in)
    barrier = pltpu.get_barrier_semaphore()

    @pl.loop(1, SHOTS)
    def _(step):
        pl.semaphore_signal(
            barrier, inc=1, device_id={"shot": ahead(step)}, device_id_type=pl.DeviceIdType.MESH
        )

    pl.semaphore_signal(
        barrier, inc=1, device_id={"surf": 1 - core}, device_id_type=pl.DeviceIdType.MESH
    )

    samples = traces[0]
    spectra = lax.dot_general(table_high[...], samples, NT, preferred_element_type=F32)
    spectra += lax.dot_general(table_low[...], samples, NT, preferred_element_type=F32)
    spec_out[...] = spectra[:256].reshape(SHOTS, 16, 1024).astype(BF16)
    last_out[...] = spectra[256:258].astype(BF16)

    owners = block_ids[...]
    earlier = (
        lax.broadcasted_iota(jnp.int32, (PART, PART), 0)
        < lax.broadcasted_iota(jnp.int32, (PART, PART), 1)
    ).astype(F32).astype(BF16)
    for index in range(PARTS):
        lanes = slice(index * PART, (index + 1) * PART)
        owner = owners[:, lanes]
        hit = owner == lax.broadcasted_iota(jnp.int32, (SHOTS, PART), 0)
        before = jnp.dot(hit.astype(F32).astype(BF16), earlier, preferred_element_type=F32)
        rank = jnp.sum(jnp.where(hit, before, 0.0), axis=0, keepdims=True).astype(jnp.int32)
        place = rank + index * CAP
        meta_out[:, lanes] = (
            (owner * 128 + place) * 4096 + shot_ids[:, lanes] * 256 + point_ids[:, lanes]
        )

    pl.semaphore_wait(barrier, SHOTS)

    def send_spec(step):
        peer = ahead(step)
        return (
            remote(spec_out.at[peer], spec_in.at[me], spec_send.at[step], spec_recv.at[me], shot=peer),
            remote(meta_out, meta_in.at[me], meta_send.at[step], meta_recv.at[me], shot=peer),
        )

    def send_last():
        return remote(last_out, last_in.at[me], last_send.at[0], last_recv.at[me], shot=0)

    own_copies = (
        pltpu.make_async_copy(spec_out.at[me], spec_in.at[me], spec_recv.at[me]),
        pltpu.make_async_copy(meta_out, meta_in.at[me], meta_recv.at[me]),
    )
    own_last = pltpu.make_async_copy(last_out, last_in.at[me], last_recv.at[me])

    @pl.loop(1, SHOTS)
    def _(step):
        for copy in send_spec(step):
            copy.start()

    for copy in own_copies:
        copy.start()

    @pl.when(me == 0)
    def _():
        own_last.start()

    @pl.when(me != 0)
    def _():
        send_last().start()

    def rows_of(index):
        return pl.ds(pl.multiple_of(index * 16, 16), 16)

    def send_recv(freq, step):
        peer = ahead(step)
        return remote(
            recv.at[peer * SPAN + freq], points.at[freq, :, rows_of(me), :],
            recv_send.at[freq], recv_recv.at[freq], shot=peer,
        )

    def own_recv(source, freq):
        return pltpu.make_async_copy(
            recv.at[source], points.at[freq, :, rows_of(me), :], recv_recv.at[freq]
        )

    def send_recv_last():
        return remote(
            recv.at[SHOTS * SPAN], points.at[SPAN, :, rows_of(me), :],
            recv_send.at[SPAN], recv_recv.at[SPAN], shot=0,
        )

    @pl.loop(0, SPAN)
    def _(freq):
        own_recv(me * SPAN + freq, freq).start()

        @pl.loop(1, SHOTS)
        def _(step):
            send_recv(freq, step).start()

    @pl.when(me == 0)
    def _():
        own_recv(SHOTS * SPAN, SPAN).start()

    @pl.when(me != 0)
    def _():
        send_recv_last().start()

    @pl.loop(0, SHOTS)
    def _(step):
        source = behind(step)
        pltpu.make_async_copy(spec_in.at[source], spec_in.at[source], spec_recv.at[source]).wait()
        pltpu.make_async_copy(meta_in.at[source], meta_in.at[source], meta_recv.at[source]).wait()

        @pl.when(me == 0)
        def _():
            pltpu.make_async_copy(last_in.at[source], last_in.at[source], last_recv.at[source]).wait()

        meta = meta_in[source]
        owner = meta // (128 * 4096)
        place = meta // 4096 % 128
        shot = (meta // 256 % 16 + 1).astype(F32)
        point = (meta % 256).astype(F32)
        values = spec_in[source].astype(F32)
        final_values = last_in[source].astype(F32)
        hit = owner == lax.broadcasted_iota(jnp.int32, (SHOTS, 1024), 0)
        lines = [jnp.where(owner == block, values, 0.0).astype(BF16) for block in range(SHOTS)]
        for line in (final_values[0:1], final_values[1:2], shot, point):
            lines.append(jnp.where(hit, line, 0.0).astype(BF16))
        target = (place == lax.broadcasted_iota(jnp.int32, (PART, 1024), 0)).astype(F32).astype(BF16)
        routed = lax.dot_general(
            jnp.concatenate(lines, axis=0), target, NT, preferred_element_type=F32
        )
        lanes = pl.ds(pl.multiple_of(source * PART, PART), PART)
        slots[:, :, lanes] = routed[:256].reshape(SHOTS, 16, PART)
        extras[:, :, lanes] = routed[256:].reshape(4, SHOTS, PART)

    @pl.loop(0, SHOTS)
    def _(block):
        row = pl.ds(block, 1)
        shot_hit = extras[2, row, :] == (
            lax.broadcasted_iota(jnp.int32, (16, 2048), 0) + 1
        ).astype(F32)
        lines = [
            jnp.where(shot_hit, slots[block, line : line + 1, :], 0.0).astype(BF16)
            for line in range(16)
        ]
        lines += [jnp.where(shot_hit, extras[line, row, :], 0.0).astype(BF16) for line in (0, 1)]
        lines.append(shot_hit.astype(F32).astype(BF16))
        point_hit = (
            extras[3, row, :] == lax.broadcasted_iota(jnp.int32, (POINTS, 2048), 0).astype(F32)
        ).astype(F32).astype(BF16)
        sums = lax.dot_general(
            jnp.concatenate(lines, axis=0), point_hit, NT, preferred_element_type=F32
        )
        scale = 1.0 / jnp.maximum(sums[288:304], 1.0)
        panel[:, rows_of(block), :] = (
            sums[:288].reshape(18, 16, POINTS) * scale[None]
        ).astype(BF16)

    def swap(freq):
        return remote(
            part.at[freq, 1 - core], other.at[freq], swap_send.at[freq], swap_recv.at[freq],
            surf=1 - core,
        )

    def multiply(freq):
        pltpu.make_async_copy(points.at[freq], points.at[freq], recv_recv.at[freq]).wait()
        both = jnp.concatenate([points[freq, 0], points[freq, 1]], axis=1)
        shots = panel[pl.ds(2 * freq, 2)].reshape(512, POINTS)
        terms = jnp.dot(shots, both, preferred_element_type=F32)
        real = terms[:256, :RCV] - terms[256:, RCV:]
        imag = terms[:256, RCV:] + terms[256:, :RCV]
        for index, value in enumerate((real, imag)):
            split = value.reshape(SHOTS, 2, 8, RCV)
            for half in range(2):
                part[freq, half, index] = split[:, half].astype(BF16)
        swap(freq).start()

    def send_out(freq, step):
        peer = ahead(step)
        return remote(
            final.at[freq, :, peer], out.at[me * SPAN + freq], out_send.at[freq], out_recv.at[0],
            shot=peer,
        )

    def send_out_last(step):
        peer = ahead(step)
        return remote(
            final.at[SPAN, :, peer], out.at[SHOTS * SPAN], out_send.at[SPAN], out_recv.at[0],
            shot=peer,
        )

    def combine(freq):
        swap(freq).wait()
        total = part[freq, core].astype(F32) + other[freq].astype(F32)
        final[freq] = total.astype(BF16)

    def finish(freq):
        combine(freq)
        pltpu.make_async_copy(final.at[freq, :, me], out.at[me * SPAN + freq], out_recv.at[0]).start()

        @pl.loop(1, SHOTS)
        def _(step):
            send_out(freq, step).start()

    multiply(0)

    @pl.loop(1, SPAN)
    def _(freq):
        multiply(freq)
        finish(freq - 1)

    @pl.when(me == 0)
    def _():
        multiply(SPAN)

    finish(SPAN - 1)

    @pl.when(me == 0)
    def _():
        combine(SPAN)
        pltpu.make_async_copy(final.at[SPAN, :, me], out.at[SHOTS * SPAN], out_recv.at[0]).start()

        @pl.loop(1, SHOTS)
        def _(step):
            send_out_last(step).start()

        sent = final.at[SPAN, :, pl.ds(0, SHOTS - 1)]
        pltpu.make_async_copy(sent, sent, out_send.at[SPAN]).wait()

    @pl.loop(1, SHOTS)
    def _(step):
        for copy in send_spec(step):
            copy.wait_send()

    @pl.when(me != 0)
    def _():
        send_last().wait_send()
        send_recv_last().wait_send()

    @pl.loop(0, SPAN)
    def _(freq):
        sent = points.at[freq, :, pl.ds(0, 240), :]
        pltpu.make_async_copy(sent, sent, recv_send.at[freq]).wait()
        sent = final.at[freq, :, pl.ds(0, SHOTS - 1)]
        pltpu.make_async_copy(sent, sent, out_send.at[freq]).wait()

    pltpu.make_async_copy(out, out, out_recv.at[0]).wait()


def local(traces, trace_block, trace_shot, trace_point, recv_panel):
    rows, window = traces.shape[1:]
    freqs = recv_panel.shape[0]
    high, low = transform_table(window, freqs)
    vmem = pl.BlockSpec(memory_space=pltpu.VMEM)
    hbm = pl.BlockSpec(memory_space=pl.ANY)
    dma = pltpu.SemaphoreType.DMA
    return pl.pallas_call(
        kernel,
        out_shape=jax.ShapeDtypeStruct((freqs, 2, 8, RCV), BF16),
        in_specs=[vmem] * 6 + [hbm],
        out_specs=hbm,
        scratch_shapes=[
            pltpu.VMEM((SHOTS, 16, rows), BF16),
            pltpu.VMEM((SHOTS, 16, rows), BF16),
            pltpu.VMEM((2, rows), BF16),
            pltpu.VMEM((SHOTS, 2, rows), BF16),
            pltpu.VMEM((1, rows), jnp.int32),
            pltpu.VMEM((SHOTS, 1, rows), jnp.int32),
            pltpu.VMEM((SHOTS, 16, 2048), F32),
            pltpu.VMEM((4, SHOTS, 2048), F32),
            pltpu.VMEM((18, 256, POINTS), BF16),
            pltpu.VMEM((SPAN + 1, 2, POINTS, RCV), BF16),
            pltpu.VMEM((SPAN + 1, 2, 2, SHOTS, 8, RCV), BF16),
            pltpu.VMEM((SPAN + 1, 2, SHOTS, 8, RCV), BF16),
            pltpu.VMEM((SPAN + 1, 2, SHOTS, 8, RCV), BF16),
            dma((SHOTS,)), dma((SHOTS,)), dma((1,)), dma((SHOTS,)), dma((SHOTS,)), dma((SHOTS,)),
            dma((SPAN + 1,)), dma((SPAN + 1,)), dma((SPAN + 1,)), dma((SPAN + 1,)),
            dma((SPAN + 1,)), dma((1,)),
        ],
        compiler_params=pltpu.CompilerParams(collective_id=0, has_side_effects=True),
        name="multiples",
    )(
        traces, trace_block.reshape(1, rows), trace_shot, trace_point,
        jnp.asarray(high), jnp.asarray(low), recv_panel,
    )


def solution(mesh):
    in_specs = (
        P("surf", "shot", None),
        P("surf", "shot", None),
        P("surf", "shot"),
        P("surf", "shot"),
        P(None, None, ("shot", "surf"), "rcv"),
    )
    out_specs = P(None, None, ("shot", "surf"), "rcv")
    return jax.shard_map(local, mesh=mesh, in_specs=in_specs, out_specs=out_specs, check_vma=False)
```

```python
import math

import jax
import jax.numpy as jnp
import numpy as np
from jax import lax
from jax.experimental import pallas as pl
from jax.experimental.pallas import tpu as pltpu
from jax.sharding import PartitionSpec as P

SHOTS = 16
SPAN = 8
PART = 128
ROWS = 256
QUARTERS = 4
CAP = 16
POINTS = 256
RCV = 128
F32 = jnp.float32
BF16 = jnp.bfloat16
NT = (((1,), (1,)), ((), ()))


def transform_table(window, freqs):
    phase = (np.arange(freqs)[:, None] * np.arange(window)[None, :] % window) * (2 * math.pi / window)
    table = np.zeros((2 * freqs + 6, window), np.float32)
    table[0 : 2 * freqs : 2] = np.cos(phase) / math.sqrt(window)
    table[1 : 2 * freqs : 2] = -np.sin(phase) / math.sqrt(window)
    high = table.astype(BF16)
    return high, (table - high.astype(np.float32)).astype(BF16)


def kernel(
    traces, block_ids, shot_ids, point_ids, table_high, table_low, recv, out,
    samples, high, low, ids, spec_out, spec_all, last_out, last_all, meta_out, meta_all,
    slots, extras, panel, points, part, other, final,
    load_sem, spec_send, spec_recv, last_send, last_recv, meta_send, meta_recv,
    gather_send, gather_recv,
    recv_send, recv_recv, swap_send, swap_recv, out_send, out_recv,
):
    me = lax.axis_index("shot")
    mine = lax.axis_index("rcv") // 2
    side = lax.axis_index("rcv") % 2
    core = lax.axis_index("surf")
    column, ring = me // 8, me % 8

    def ahead(step):
        return (column + step % 2) % 2 * 8 + (ring + step // 2) % 8

    def beside(step):
        return (mine + step) % QUARTERS * 2 + side

    def remote(src, dst, send, arrive, **where):
        return pltpu.make_async_remote_copy(
            src_ref=src, dst_ref=dst, send_sem=send, recv_sem=arrive,
            device_id=where, device_id_type=pl.DeviceIdType.MESH,
        )

    lanes = pl.ds(pl.multiple_of(mine * ROWS, ROWS), ROWS)
    loads = [
        pltpu.make_async_copy(traces.at[0, lanes, :], samples, load_sem.at[0]),
        pltpu.make_async_copy(table_high, high, load_sem.at[1]),
        pltpu.make_async_copy(table_low, low, load_sem.at[2]),
        pltpu.make_async_copy(block_ids.at[:, lanes], ids.at[0], load_sem.at[3]),
        pltpu.make_async_copy(shot_ids.at[:, lanes], ids.at[1], load_sem.at[4]),
        pltpu.make_async_copy(point_ids.at[:, lanes], ids.at[2], load_sem.at[5]),
    ]
    for load in loads:
        load.start()

    last_all[...] = jnp.zeros_like(last_all)
    barrier = pltpu.get_barrier_semaphore()

    @pl.loop(1, SHOTS)
    def _(step):
        pl.semaphore_signal(
            barrier, inc=1, device_id={"shot": ahead(step)}, device_id_type=pl.DeviceIdType.MESH
        )

    @pl.loop(1, QUARTERS)
    def _(step):
        pl.semaphore_signal(
            barrier, inc=1, device_id={"rcv": beside(step)}, device_id_type=pl.DeviceIdType.MESH
        )

    pl.semaphore_signal(
        barrier, inc=1, device_id={"surf": 1 - core}, device_id_type=pl.DeviceIdType.MESH
    )
    for load in loads:
        load.wait()

    spectra = lax.dot_general(high[...], samples[...], NT, preferred_element_type=F32)
    spectra += lax.dot_general(low[...], samples[...], NT, preferred_element_type=F32)
    spec_out[...] = spectra[:256].reshape(SHOTS, 16, ROWS).astype(BF16)
    last_out[...] = spectra[256:258].astype(BF16)

    earlier = (
        lax.broadcasted_iota(jnp.int32, (PART, PART), 0)
        < lax.broadcasted_iota(jnp.int32, (PART, PART), 1)
    ).astype(F32).astype(BF16)
    for index in range(ROWS // PART):
        half = slice(index * PART, (index + 1) * PART)
        owner = ids[0, :, half]
        hits = owner == lax.broadcasted_iota(jnp.int32, (SHOTS, PART), 0)
        before = jnp.dot(hits.astype(F32).astype(BF16), earlier, preferred_element_type=F32)
        rank = jnp.sum(jnp.where(hits, before, 0.0), axis=0, keepdims=True).astype(jnp.int32)
        place = (me % 8 * 2 + index) * CAP + rank
        meta_out[:, half] = (owner * 256 + place) * 4096 + ids[1, :, half] * 256 + ids[2, :, half]

    pl.semaphore_wait(barrier, SHOTS - 1 + QUARTERS - 1 + 1)

    def send_spec(step):
        peer = ahead(step)
        return (
            remote(spec_out.at[peer], spec_all.at[mine, me], spec_send.at[step], spec_recv.at[0], shot=peer),
            remote(meta_out, meta_all.at[mine, me], meta_send.at[step], meta_recv.at[0], shot=peer),
        )

    def send_last():
        return remote(last_out, last_all.at[mine, me], last_send.at[0], last_recv.at[0], shot=0)

    @pl.loop(1, SHOTS)
    def _(step):
        for copy in send_spec(step):
            copy.start()

    pltpu.make_async_copy(spec_out.at[me], spec_all.at[mine, me], spec_recv.at[0]).start()
    pltpu.make_async_copy(meta_out, meta_all.at[mine, me], meta_recv.at[0]).start()

    @pl.when(me == 0)
    def _():
        pltpu.make_async_copy(last_out, last_all.at[mine, me], last_recv.at[0]).start()

    @pl.when(me != 0)
    def _():
        send_last().start()

    def rows_of(index):
        return pl.ds(pl.multiple_of(index * 16, 16), 16)

    def send_recv(freq, step):
        peer = ahead(step)
        return remote(
            recv.at[peer * SPAN + freq], points.at[freq, :, rows_of(me), :],
            recv_send.at[freq], recv_recv.at[freq], shot=peer,
        )

    def own_recv(source, freq):
        return pltpu.make_async_copy(
            recv.at[source], points.at[freq, :, rows_of(me), :], recv_recv.at[freq]
        )

    def send_recv_last():
        return remote(
            recv.at[SHOTS * SPAN], points.at[SPAN, :, rows_of(me), :],
            recv_send.at[SPAN], recv_recv.at[SPAN], shot=0,
        )

    @pl.loop(0, SPAN)
    def _(freq):
        own_recv(me * SPAN + freq, freq).start()

        @pl.loop(1, SHOTS)
        def _(step):
            send_recv(freq, step).start()

    @pl.when(me == 0)
    def _():
        own_recv(SHOTS * SPAN, SPAN).start()

    @pl.when(me != 0)
    def _():
        send_recv_last().start()

    def arrived(buffer, index, sem):
        whole = buffer.at[index]
        pltpu.make_async_copy(whole, whole, sem).wait()

    def gather(kind, buffer, step):
        return remote(
            buffer.at[mine], buffer.at[mine], gather_send.at[kind, step], gather_recv.at[kind, step],
            rcv=beside(step),
        )

    arrived(spec_all, mine, spec_recv.at[0])
    arrived(meta_all, mine, meta_recv.at[0])

    @pl.when(me == 0)
    def _():
        arrived(last_all, mine, last_recv.at[0])

    @pl.loop(1, QUARTERS)
    def _(step):
        gather(0, spec_all, step).start()
        gather(1, meta_all, step).start()

        @pl.when(me == 0)
        def _():
            gather(2, last_all, step).start()

    def place_rows(index, group):
        sources = [group * 8 + source for source in range(8)]
        meta = jnp.concatenate([meta_all[index, source] for source in sources], axis=1)
        values = jnp.concatenate([spec_all[index, source] for source in sources], axis=1)
        final_values = jnp.concatenate([last_all[index, source] for source in sources], axis=1)
        values, final_values = values.astype(F32), final_values.astype(F32)
        owner = meta // (256 * 4096)
        place = meta // 4096 % 256
        shot = (meta // 256 % 16 + 1).astype(F32)
        point = (meta % 256).astype(F32)
        hit = owner == lax.broadcasted_iota(jnp.int32, (SHOTS, 2048), 0)
        lines = [jnp.where(owner == block, values, 0.0).astype(BF16) for block in range(SHOTS)]
        for line in (final_values[0:1], final_values[1:2], shot, point):
            lines.append(jnp.where(hit, line, 0.0).astype(BF16))
        target = (place == lax.broadcasted_iota(jnp.int32, (256, 2048), 0)).astype(F32).astype(BF16)
        routed = lax.dot_general(
            jnp.concatenate(lines, axis=0), target, NT, preferred_element_type=F32
        )
        places = pl.ds(pl.multiple_of((index * 2 + group) * 256, 256), 256)
        slots[:, :, places] = routed[:256].reshape(SHOTS, 16, 256)
        extras[:, :, places] = routed[256:].reshape(4, SHOTS, 256)

    @pl.loop(0, 2)
    def _(group):
        place_rows(mine, group)

    @pl.loop(1, QUARTERS)
    def _(step):
        index = (mine + QUARTERS - step) % QUARTERS
        arrived(spec_all, index, gather_recv.at[0, step])
        arrived(meta_all, index, gather_recv.at[1, step])

        @pl.when(me == 0)
        def _():
            arrived(last_all, index, gather_recv.at[2, step])

        @pl.loop(0, 2)
        def _(group):
            place_rows(index, group)

    @pl.loop(0, SHOTS, unroll=4)
    def _(block):
        line_of = pl.ds(block, 1)
        shot_hit = extras[2, line_of, :] == (
            lax.broadcasted_iota(jnp.int32, (16, 2048), 0) + 1
        ).astype(F32)
        lines = [
            jnp.where(shot_hit, slots[block, line : line + 1, :], 0.0).astype(BF16)
            for line in range(16)
        ]
        lines += [jnp.where(shot_hit, extras[line, line_of, :], 0.0).astype(BF16) for line in (0, 1)]
        lines.append(shot_hit.astype(F32).astype(BF16))
        point_hit = (
            extras[3, line_of, :] == lax.broadcasted_iota(jnp.int32, (POINTS, 2048), 0).astype(F32)
        ).astype(F32).astype(BF16)
        sums = lax.dot_general(
            jnp.concatenate(lines, axis=0), point_hit, NT, preferred_element_type=F32
        )
        scale = 1.0 / jnp.maximum(sums[288:304], 1.0)
        panel[:, rows_of(block), :] = (
            sums[:288].reshape(18, 16, POINTS) * scale[None]
        ).astype(BF16)

    def swap(freq):
        return remote(
            part.at[freq, 1 - core], other.at[freq], swap_send.at[freq], swap_recv.at[freq],
            surf=1 - core,
        )

    def multiply(freq):
        pltpu.make_async_copy(points.at[freq], points.at[freq], recv_recv.at[freq]).wait()
        both = jnp.concatenate([points[freq, 0], points[freq, 1]], axis=1)
        shots = panel[pl.ds(2 * freq, 2)].reshape(512, POINTS)
        terms = jnp.dot(shots, both, preferred_element_type=F32)
        real = terms[:256, :RCV] - terms[256:, RCV:]
        imag = terms[:256, RCV:] + terms[256:, :RCV]
        for index, value in enumerate((real, imag)):
            split = value.reshape(SHOTS, 2, 8, RCV)
            for half in range(2):
                part[freq, half, index] = split[:, half].astype(BF16)
        swap(freq).start()

    def send_out(freq, step):
        peer = ahead(step)
        return remote(
            final.at[freq, :, peer], out.at[me * SPAN + freq], out_send.at[freq], out_recv.at[0],
            shot=peer,
        )

    def send_out_last(step):
        peer = ahead(step)
        return remote(
            final.at[SPAN, :, peer], out.at[SHOTS * SPAN], out_send.at[SPAN], out_recv.at[0],
            shot=peer,
        )

    def combine(freq):
        swap(freq).wait()
        total = part[freq, core].astype(F32) + other[freq].astype(F32)
        final[freq] = total.astype(BF16)

    def finish(freq):
        combine(freq)
        pltpu.make_async_copy(final.at[freq, :, me], out.at[me * SPAN + freq], out_recv.at[0]).start()

        @pl.loop(1, SHOTS)
        def _(step):
            send_out(freq, step).start()

    multiply(0)

    @pl.loop(1, SPAN)
    def _(freq):
        multiply(freq)
        finish(freq - 1)

    @pl.when(me == 0)
    def _():
        multiply(SPAN)

    finish(SPAN - 1)

    @pl.when(me == 0)
    def _():
        combine(SPAN)
        pltpu.make_async_copy(final.at[SPAN, :, me], out.at[SHOTS * SPAN], out_recv.at[0]).start()

        @pl.loop(1, SHOTS)
        def _(step):
            send_out_last(step).start()

        sent = final.at[SPAN, :, pl.ds(0, SHOTS - 1)]
        pltpu.make_async_copy(sent, sent, out_send.at[SPAN]).wait()

    @pl.loop(1, SHOTS)
    def _(step):
        for copy in send_spec(step):
            copy.wait_send()

    @pl.loop(1, QUARTERS)
    def _(step):
        gather(0, spec_all, step).wait_send()
        gather(1, meta_all, step).wait_send()

        @pl.when(me == 0)
        def _():
            gather(2, last_all, step).wait_send()

    @pl.when(me != 0)
    def _():
        send_last().wait_send()
        send_recv_last().wait_send()

    @pl.loop(0, SPAN)
    def _(freq):
        sent = points.at[freq, :, pl.ds(0, 240), :]
        pltpu.make_async_copy(sent, sent, recv_send.at[freq]).wait()
        sent = final.at[freq, :, pl.ds(0, SHOTS - 1)]
        pltpu.make_async_copy(sent, sent, out_send.at[freq]).wait()

    pltpu.make_async_copy(out, out, out_recv.at[0]).wait()


def local(traces, trace_block, trace_shot, trace_point, recv_panel):
    rows, window = traces.shape[1:]
    freqs = recv_panel.shape[0]
    high, low = transform_table(window, freqs)
    hbm = pl.BlockSpec(memory_space=pltpu.HBM)
    dma = pltpu.SemaphoreType.DMA
    return pl.pallas_call(
        kernel,
        out_shape=jax.ShapeDtypeStruct((freqs, 2, 8, RCV), BF16),
        in_specs=[hbm] * 7,
        out_specs=pl.BlockSpec(memory_space=pl.ANY),
        scratch_shapes=[
            pltpu.VMEM((ROWS, window), BF16),
            pltpu.VMEM(high.shape, BF16),
            pltpu.VMEM(low.shape, BF16),
            pltpu.VMEM((3, 1, ROWS), jnp.int32),
            pltpu.VMEM((SHOTS, 16, ROWS), BF16),
            pltpu.VMEM((QUARTERS, SHOTS, 16, ROWS), BF16),
            pltpu.VMEM((2, ROWS), BF16),
            pltpu.VMEM((QUARTERS, SHOTS, 2, ROWS), BF16),
            pltpu.VMEM((1, ROWS), jnp.int32),
            pltpu.VMEM((QUARTERS, SHOTS, 1, ROWS), jnp.int32),
            pltpu.VMEM((SHOTS, 16, 2048), F32),
            pltpu.VMEM((4, SHOTS, 2048), F32),
            pltpu.VMEM((18, 256, POINTS), BF16),
            pltpu.VMEM((SPAN + 1, 2, POINTS, RCV), BF16),
            pltpu.VMEM((SPAN + 1, 2, 2, SHOTS, 8, RCV), BF16),
            pltpu.VMEM((SPAN + 1, 2, SHOTS, 8, RCV), BF16),
            pltpu.VMEM((SPAN + 1, 2, SHOTS, 8, RCV), BF16),
            dma((6,)), dma((SHOTS,)), dma((1,)), dma((1,)), dma((1,)), dma((SHOTS,)), dma((1,)),
            dma((3, QUARTERS)), dma((3, QUARTERS)),
            dma((SPAN + 1,)), dma((SPAN + 1,)), dma((SPAN + 1,)), dma((SPAN + 1,)),
            dma((SPAN + 1,)), dma((1,)),
        ],
        compiler_params=pltpu.CompilerParams(collective_id=0, has_side_effects=True),
        name="multiples",
    )(
        traces, trace_block.reshape(1, rows), trace_shot, trace_point,
        jnp.asarray(high), jnp.asarray(low), recv_panel,
    )


def solution(mesh):
    in_specs = (
        P("surf", "shot", None),
        P("surf", "shot", None),
        P("surf", "shot"),
        P("surf", "shot"),
        P(None, None, ("shot", "surf"), "rcv"),
    )
    out_specs = P(None, None, ("shot", "surf"), "rcv")
    return jax.shard_map(local, mesh=mesh, in_specs=in_specs, out_specs=out_specs, check_vma=False)
```

```python
import math

import jax
import jax.numpy as jnp
import numpy as np
from jax import lax
from jax.experimental import pallas as pl
from jax.experimental.pallas import tpu as pltpu
from jax.sharding import PartitionSpec as P

SHOTS = 16
SPAN = 8
PART = 128
PARTS = 8
CAP = 16
LAST = 15
POINTS = 256
RCV = 128
F32 = jnp.float32
BF16 = jnp.bfloat16
NT = (((1,), (1,)), ((), ()))


def transform_table(window, freqs):
    phase = (np.arange(freqs)[:, None] * np.arange(window)[None, :] % window) * (2 * math.pi / window)
    table = np.zeros((2 * freqs + 6, window), np.float32)
    table[0 : 2 * freqs : 2] = np.cos(phase) / math.sqrt(window)
    table[1 : 2 * freqs : 2] = -np.sin(phase) / math.sqrt(window)
    high = table.astype(BF16)
    return high, (table - high.astype(np.float32)).astype(BF16)


def kernel(
    traces, block_ids, shot_ids, point_ids, table_high, table_low, recv, out,
    samples, high, low, ids, spec_out, spec_all, last_out, last_all, meta_out, meta_all,
    slots, extras, panel, points, part, other, final,
    load_sem, spec_send, spec_recv, last_send, last_recv, meta_send, meta_recv,
    gather_send, gather_recv,
    recv_send, recv_recv, swap_send, swap_recv, out_send, out_recv,
):
    me = lax.axis_index("shot")
    mine = lax.axis_index("rcv")
    row, side = mine // 2, mine % 2
    core = lax.axis_index("surf")
    column, ring = me // 8, me % 8

    def ahead(step):
        return (column + step % 2) % 2 * 8 + (ring + step // 2) % 8

    def owned(index):
        return (index // 8 + side) % 2 * 8 + index % 8

    own = owned(me)
    last_home = owned(LAST)

    def beside(step):
        return {
            "shot": (column + step % 2) % 2 * 8 + ring,
            "rcv": (row + step // 2) % 4 * 2 + (side + step % 2) % 2,
        }

    def beside_back(step):
        return (row + 4 - step // 2) % 4 * 2 + (side + step % 2) % 2

    def remote(src, dst, send, arrive, **where):
        return pltpu.make_async_remote_copy(
            src_ref=src, dst_ref=dst, send_sem=send, recv_sem=arrive,
            device_id=where, device_id_type=pl.DeviceIdType.MESH,
        )

    lanes = pl.ds(pl.multiple_of(mine * PART, PART), PART)
    loads = [
        pltpu.make_async_copy(traces.at[0, lanes, :], samples, load_sem.at[0]),
        pltpu.make_async_copy(table_high, high, load_sem.at[1]),
        pltpu.make_async_copy(table_low, low, load_sem.at[2]),
        pltpu.make_async_copy(block_ids.at[:, lanes], ids.at[0], load_sem.at[3]),
        pltpu.make_async_copy(shot_ids.at[:, lanes], ids.at[1], load_sem.at[4]),
        pltpu.make_async_copy(point_ids.at[:, lanes], ids.at[2], load_sem.at[5]),
    ]
    for load in loads:
        load.start()

    last_all[...] = jnp.zeros_like(last_all)
    barrier = pltpu.get_barrier_semaphore()

    @pl.loop(1, SHOTS)
    def _(step):
        pl.semaphore_signal(
            barrier, inc=1, device_id={"shot": ahead(step)}, device_id_type=pl.DeviceIdType.MESH
        )

    @pl.loop(1, PARTS)
    def _(step):
        pl.semaphore_signal(
            barrier, inc=1, device_id=beside(step), device_id_type=pl.DeviceIdType.MESH
        )

    pl.semaphore_signal(
        barrier, inc=1, device_id={"surf": 1 - core}, device_id_type=pl.DeviceIdType.MESH
    )
    for load in loads:
        load.wait()

    spectra = lax.dot_general(high[...], samples[...], NT, preferred_element_type=F32)
    spectra += lax.dot_general(low[...], samples[...], NT, preferred_element_type=F32)
    spec_out[...] = spectra[:256].reshape(SHOTS, 16, PART).astype(BF16)
    last_out[...] = spectra[256:258].astype(BF16)

    earlier = (
        lax.broadcasted_iota(jnp.int32, (PART, PART), 0)
        < lax.broadcasted_iota(jnp.int32, (PART, PART), 1)
    ).astype(F32).astype(BF16)
    owners = ids[0]
    hits = owners == lax.broadcasted_iota(jnp.int32, (SHOTS, PART), 0)
    before = jnp.dot(hits.astype(F32).astype(BF16), earlier, preferred_element_type=F32)
    rank = jnp.sum(jnp.where(hits, before, 0.0), axis=0, keepdims=True).astype(jnp.int32)
    meta_out[...] = (owners * 256 + me * CAP + rank) * 4096 + ids[1] * 256 + ids[2]

    pl.semaphore_wait(barrier, SHOTS - 1 + PARTS - 1 + 1)

    def send_spec(step):
        peer = ahead(step)
        return (
            remote(spec_out.at[owned(peer)], spec_all.at[mine, me], spec_send.at[step], spec_recv.at[0], shot=peer),
            remote(meta_out, meta_all.at[mine, me], meta_send.at[step], meta_recv.at[0], shot=peer),
        )

    def send_last():
        return remote(last_out, last_all.at[mine, me], last_send.at[0], last_recv.at[0], shot=last_home)

    @pl.loop(1, SHOTS)
    def _(step):
        for copy in send_spec(step):
            copy.start()

    pltpu.make_async_copy(spec_out.at[own], spec_all.at[mine, me], spec_recv.at[0]).start()
    pltpu.make_async_copy(meta_out, meta_all.at[mine, me], meta_recv.at[0]).start()

    @pl.when(own == LAST)
    def _():
        pltpu.make_async_copy(last_out, last_all.at[mine, me], last_recv.at[0]).start()

    @pl.when(own != LAST)
    def _():
        send_last().start()

    def rows_of(index):
        return pl.ds(pl.multiple_of(index * 16, 16), 16)

    def send_recv(freq, step):
        peer = ahead(step)
        return remote(
            recv.at[owned(peer) * SPAN + freq], points.at[freq, :, rows_of(me), :],
            recv_send.at[freq], recv_recv.at[freq], shot=peer,
        )

    def own_recv(source, freq):
        return pltpu.make_async_copy(
            recv.at[source], points.at[freq, :, rows_of(me), :], recv_recv.at[freq]
        )

    def send_recv_last():
        return remote(
            recv.at[SHOTS * SPAN], points.at[SPAN, :, rows_of(me), :],
            recv_send.at[SPAN], recv_recv.at[SPAN], shot=last_home,
        )

    @pl.when(own == LAST)
    def _():
        own_recv(SHOTS * SPAN, SPAN).start()

    @pl.when(own != LAST)
    def _():
        send_recv_last().start()

    @pl.loop(0, SPAN)
    def _(freq):
        own_recv(own * SPAN + freq, freq).start()

        @pl.loop(1, SHOTS)
        def _(step):
            send_recv(freq, step).start()

    def arrived(buffer, index, sem):
        whole = buffer.at[index]
        pltpu.make_async_copy(whole, whole, sem).wait()

    def gather(kind, buffer, step):
        return remote(
            buffer.at[mine], buffer.at[mine], gather_send.at[kind, step], gather_recv.at[kind, step],
            **beside(step),
        )

    arrived(spec_all, mine, spec_recv.at[0])
    arrived(meta_all, mine, meta_recv.at[0])

    @pl.when(own == LAST)
    def _():
        arrived(last_all, mine, last_recv.at[0])

    @pl.loop(1, PARTS)
    def _(step):
        gather(0, spec_all, step).start()
        gather(1, meta_all, step).start()

        @pl.when(own == LAST)
        def _():
            gather(2, last_all, step).start()

    def place_rows(index):
        meta = jnp.concatenate([meta_all[index, source] for source in range(SHOTS)], axis=1)
        values = jnp.concatenate([spec_all[index, source] for source in range(SHOTS)], axis=1)
        final_values = jnp.concatenate([last_all[index, source] for source in range(SHOTS)], axis=1)
        values, final_values = values.astype(F32), final_values.astype(F32)
        owner = meta // (256 * 4096)
        place = meta // 4096 % 256
        shot = (meta // 256 % 16 + 1).astype(F32)
        point = (meta % 256).astype(F32)
        hit = owner == lax.broadcasted_iota(jnp.int32, (SHOTS, 2048), 0)
        lines = [jnp.where(owner == block, values, 0.0).astype(BF16) for block in range(SHOTS)]
        for line in (final_values[0:1], final_values[1:2], shot, point):
            lines.append(jnp.where(hit, line, 0.0).astype(BF16))
        target = (place == lax.broadcasted_iota(jnp.int32, (256, 2048), 0)).astype(F32).astype(BF16)
        routed = lax.dot_general(
            jnp.concatenate(lines, axis=0), target, NT, preferred_element_type=F32
        )
        places = pl.ds(pl.multiple_of(index * 256, 256), 256)
        slots[:, :, places] = routed[:256].reshape(SHOTS, 16, 256)
        extras[:, :, places] = routed[256:].reshape(4, SHOTS, 256)

    place_rows(mine)

    @pl.loop(1, PARTS)
    def _(step):
        index = beside_back(step)
        arrived(spec_all, index, gather_recv.at[0, step])
        arrived(meta_all, index, gather_recv.at[1, step])

        @pl.when(own == LAST)
        def _():
            arrived(last_all, index, gather_recv.at[2, step])

        place_rows(index)

    @pl.loop(0, SHOTS, unroll=8)
    def _(block):
        line_of = pl.ds(block, 1)
        shot_hit = extras[2, line_of, :] == (
            lax.broadcasted_iota(jnp.int32, (16, 2048), 0) + 1
        ).astype(F32)
        lines = [
            jnp.where(shot_hit, slots[block, line : line + 1, :], 0.0).astype(BF16)
            for line in range(16)
        ]
        lines += [jnp.where(shot_hit, extras[line, line_of, :], 0.0).astype(BF16) for line in (0, 1)]
        lines.append(shot_hit.astype(F32).astype(BF16))
        point_hit = (
            extras[3, line_of, :] == lax.broadcasted_iota(jnp.int32, (POINTS, 2048), 0).astype(F32)
        ).astype(F32).astype(BF16)
        sums = lax.dot_general(
            jnp.concatenate(lines, axis=0), point_hit, NT, preferred_element_type=F32
        )
        scale = 1.0 / jnp.maximum(sums[288:304], 1.0)
        panel[:, rows_of(block), :] = (
            sums[:288].reshape(18, 16, POINTS) * scale[None]
        ).astype(BF16)

    def swap(freq):
        return remote(
            part.at[freq, 1 - core], other.at[freq], swap_send.at[freq], swap_recv.at[freq],
            surf=1 - core,
        )

    def multiply(freq):
        pltpu.make_async_copy(points.at[freq], points.at[freq], recv_recv.at[freq]).wait()
        both = jnp.concatenate([points[freq, 0], points[freq, 1]], axis=1)
        shots = panel[pl.ds(2 * freq, 2)].reshape(512, POINTS)
        terms = jnp.dot(shots, both, preferred_element_type=F32)
        real = terms[:256, :RCV] - terms[256:, RCV:]
        imag = terms[:256, RCV:] + terms[256:, :RCV]
        for index, value in enumerate((real, imag)):
            split = value.reshape(SHOTS, 2, 8, RCV)
            for half in range(2):
                part[freq, half, index] = split[:, half].astype(BF16)
        swap(freq).start()

    def send_out(freq, step):
        peer = ahead(step)
        return remote(
            final.at[freq, :, peer], out.at[own * SPAN + freq], out_send.at[freq], out_recv.at[0],
            shot=peer,
        )

    def send_out_last(step):
        peer = ahead(step)
        return remote(
            final.at[SPAN, :, peer], out.at[SHOTS * SPAN], out_send.at[SPAN], out_recv.at[0],
            shot=peer,
        )

    def combine(freq):
        swap(freq).wait()
        total = part[freq, core].astype(F32) + other[freq].astype(F32)
        final[freq] = total.astype(BF16)

    def finish(freq):
        combine(freq)
        pltpu.make_async_copy(final.at[freq, :, me], out.at[own * SPAN + freq], out_recv.at[0]).start()

        @pl.loop(1, SHOTS)
        def _(step):
            send_out(freq, step).start()

    @pl.when(own == LAST)
    def _():
        multiply(SPAN)

    multiply(0)

    @pl.when(own == LAST)
    def _():
        combine(SPAN)
        pltpu.make_async_copy(final.at[SPAN, :, me], out.at[SHOTS * SPAN], out_recv.at[0]).start()

        @pl.loop(1, SHOTS)
        def _(step):
            send_out_last(step).start()

    @pl.loop(1, SPAN)
    def _(freq):
        multiply(freq)
        finish(freq - 1)

    finish(SPAN - 1)

    @pl.loop(1, SHOTS)
    def _(step):
        for copy in send_spec(step):
            copy.wait_send()

    @pl.loop(1, PARTS)
    def _(step):
        gather(0, spec_all, step).wait_send()
        gather(1, meta_all, step).wait_send()

        @pl.when(own == LAST)
        def _():
            gather(2, last_all, step).wait_send()

    @pl.when(own != LAST)
    def _():
        send_last().wait_send()
        send_recv_last().wait_send()

    @pl.loop(0, SPAN)
    def _(freq):
        sent = points.at[freq, :, pl.ds(0, 240), :]
        pltpu.make_async_copy(sent, sent, recv_send.at[freq]).wait()
        sent = final.at[freq, :, pl.ds(0, SHOTS - 1)]
        pltpu.make_async_copy(sent, sent, out_send.at[freq]).wait()

    @pl.when(own == LAST)
    def _():
        sent = final.at[SPAN, :, pl.ds(0, SHOTS - 1)]
        pltpu.make_async_copy(sent, sent, out_send.at[SPAN]).wait()

    pltpu.make_async_copy(out, out, out_recv.at[0]).wait()


def local(traces, trace_block, trace_shot, trace_point, recv_panel):
    rows, window = traces.shape[1:]
    freqs = recv_panel.shape[0]
    high, low = transform_table(window, freqs)
    hbm = pl.BlockSpec(memory_space=pltpu.HBM)
    dma = pltpu.SemaphoreType.DMA
    return pl.pallas_call(
        kernel,
        out_shape=jax.ShapeDtypeStruct((freqs, 2, 8, RCV), BF16),
        in_specs=[hbm] * 7,
        out_specs=pl.BlockSpec(memory_space=pl.ANY),
        scratch_shapes=[
            pltpu.VMEM((PART, window), BF16),
            pltpu.VMEM(high.shape, BF16),
            pltpu.VMEM(low.shape, BF16),
            pltpu.VMEM((3, 1, PART), jnp.int32),
            pltpu.VMEM((SHOTS, 16, PART), BF16),
            pltpu.VMEM((PARTS, SHOTS, 16, PART), BF16),
            pltpu.VMEM((2, PART), BF16),
            pltpu.VMEM((PARTS, SHOTS, 2, PART), BF16),
            pltpu.VMEM((1, PART), jnp.int32),
            pltpu.VMEM((PARTS, SHOTS, 1, PART), jnp.int32),
            pltpu.VMEM((SHOTS, 16, 2048), F32),
            pltpu.VMEM((4, SHOTS, 2048), F32),
            pltpu.VMEM((18, 256, POINTS), BF16),
            pltpu.VMEM((SPAN + 1, 2, POINTS, RCV), BF16),
            pltpu.VMEM((SPAN + 1, 2, 2, SHOTS, 8, RCV), BF16),
            pltpu.VMEM((SPAN + 1, 2, SHOTS, 8, RCV), BF16),
            pltpu.VMEM((SPAN + 1, 2, SHOTS, 8, RCV), BF16),
            dma((6,)), dma((SHOTS,)), dma((1,)), dma((1,)), dma((1,)), dma((SHOTS,)), dma((1,)),
            dma((3, PARTS)), dma((3, PARTS)),
            dma((SPAN + 1,)), dma((SPAN + 1,)), dma((SPAN + 1,)), dma((SPAN + 1,)),
            dma((SPAN + 1,)), dma((1,)),
        ],
        compiler_params=pltpu.CompilerParams(collective_id=0, has_side_effects=True, vmem_limit_bytes=48 * 1024 * 1024),
        name="multiples",
    )(
        *(
            pltpu.with_memory_space_constraint(array, pltpu.HBM)
            for array in (
                traces, trace_block.reshape(1, rows), trace_shot, trace_point,
                jnp.asarray(high), jnp.asarray(low), recv_panel,
            )
        )
    )


def solution(mesh):
    in_specs = (
        P("surf", "shot", None),
        P("surf", "shot", None),
        P("surf", "shot"),
        P("surf", "shot"),
        P(None, None, ("shot", "surf"), "rcv"),
    )
    out_specs = P(None, None, ("shot", "surf"), "rcv")
    return jax.shard_map(local, mesh=mesh, in_specs=in_specs, out_specs=out_specs, check_vma=False)
```

```python
import math

import jax
import jax.numpy as jnp
import numpy as np
from jax import lax
from jax.experimental import pallas as pl
from jax.experimental.pallas import tpu as pltpu
from jax.sharding import PartitionSpec as P

SHOTS = 16
SPAN = 8
PART = 128
PARTS = 8
CAP = 16
FIRST = 3
DEFER = 4
LAST = 15
POINTS = 256
RCV = 128
F32 = jnp.float32
BF16 = jnp.bfloat16
NT = (((1,), (1,)), ((), ()))


def transform_table(window, freqs):
    phase = (np.arange(freqs)[:, None] * np.arange(window)[None, :] % window) * (2 * math.pi / window)
    table = np.zeros((2 * freqs + 6, window), np.float32)
    table[0 : 2 * freqs : 2] = np.cos(phase) / math.sqrt(window)
    table[1 : 2 * freqs : 2] = -np.sin(phase) / math.sqrt(window)
    high = table.astype(BF16)
    return high, (table - high.astype(np.float32)).astype(BF16)


def kernel(
    traces, block_ids, shot_ids, point_ids, table_high, table_low, recv, out,
    samples, high, low, ids, spec_out, spec_all, last_out, last_all, meta_out, meta_all,
    slots, extras, panel, points, part, other, final,
    load_sem, spec_send, spec_recv, last_send, last_recv, meta_send, meta_recv,
    gather_send, gather_recv,
    recv_send, recv_recv, swap_send, swap_recv, out_send, out_recv,
):
    me = lax.axis_index("shot")
    mine = lax.axis_index("rcv")
    row, side = mine // 2, mine % 2
    core = lax.axis_index("surf")
    column, ring = me // 8, me % 8

    def ahead(step):
        return (column + step % 2) % 2 * 8 + (ring + step // 2) % 8

    def owned(index):
        return (index // 8 + side) % 2 * 8 + index % 8

    own = owned(me)
    last_home = owned(LAST)

    def beside(step):
        return {
            "shot": (column + step % 2) % 2 * 8 + ring,
            "rcv": (row + step // 2) % 4 * 2 + (side + step % 2) % 2,
        }

    def beside_back(step):
        return (row + 4 - step // 2) % 4 * 2 + (side + step % 2) % 2

    def remote(src, dst, send, arrive, **where):
        return pltpu.make_async_remote_copy(
            src_ref=src, dst_ref=dst, send_sem=send, recv_sem=arrive,
            device_id=where, device_id_type=pl.DeviceIdType.MESH,
        )

    lanes = pl.ds(pl.multiple_of(mine * PART, PART), PART)
    loads = [
        pltpu.make_async_copy(traces.at[0, lanes, :], samples, load_sem.at[0]),
        pltpu.make_async_copy(table_high, high, load_sem.at[1]),
        pltpu.make_async_copy(table_low, low, load_sem.at[2]),
        pltpu.make_async_copy(block_ids.at[:, lanes], ids.at[0], load_sem.at[3]),
        pltpu.make_async_copy(shot_ids.at[:, lanes], ids.at[1], load_sem.at[4]),
        pltpu.make_async_copy(point_ids.at[:, lanes], ids.at[2], load_sem.at[5]),
    ]
    for load in loads:
        load.start()

    last_all[...] = jnp.zeros_like(last_all)
    barrier = pltpu.get_barrier_semaphore()

    @pl.loop(1, SHOTS)
    def _(step):
        pl.semaphore_signal(
            barrier, inc=1, device_id={"shot": ahead(step)}, device_id_type=pl.DeviceIdType.MESH
        )

    @pl.loop(1, PARTS)
    def _(step):
        pl.semaphore_signal(
            barrier, inc=1, device_id=beside(step), device_id_type=pl.DeviceIdType.MESH
        )

    pl.semaphore_signal(
        barrier, inc=1, device_id={"surf": 1 - core}, device_id_type=pl.DeviceIdType.MESH
    )
    for load in loads:
        load.wait()

    spectra = lax.dot_general(high[...], samples[...], NT, preferred_element_type=F32)
    spectra += lax.dot_general(low[...], samples[...], NT, preferred_element_type=F32)
    spec_out[...] = spectra[:256].reshape(SHOTS, 16, PART).astype(BF16)
    last_out[...] = spectra[256:258].astype(BF16)

    earlier = (
        lax.broadcasted_iota(jnp.int32, (PART, PART), 0)
        < lax.broadcasted_iota(jnp.int32, (PART, PART), 1)
    ).astype(F32).astype(BF16)
    owners = ids[0]
    hits = owners == lax.broadcasted_iota(jnp.int32, (SHOTS, PART), 0)
    before = jnp.dot(hits.astype(F32).astype(BF16), earlier, preferred_element_type=F32)
    rank = jnp.sum(jnp.where(hits, before, 0.0), axis=0, keepdims=True).astype(jnp.int32)
    meta_out[...] = (owners * 256 + me * CAP + rank) * 4096 + ids[1] * 256 + ids[2]

    pl.semaphore_wait(barrier, SHOTS - 1 + PARTS - 1 + 1)

    def send_spec(step):
        peer = ahead(step)
        return (
            remote(spec_out.at[owned(peer)], spec_all.at[mine, me], spec_send.at[step], spec_recv.at[0], shot=peer),
            remote(meta_out, meta_all.at[mine, me], meta_send.at[step], meta_recv.at[0], shot=peer),
        )

    def send_last():
        return remote(last_out, last_all.at[mine, me], last_send.at[0], last_recv.at[0], shot=last_home)

    @pl.loop(1, SHOTS)
    def _(step):
        for copy in send_spec(step):
            copy.start()

    pltpu.make_async_copy(spec_out.at[own], spec_all.at[mine, me], spec_recv.at[0]).start()
    pltpu.make_async_copy(meta_out, meta_all.at[mine, me], meta_recv.at[0]).start()

    @pl.when(own == LAST)
    def _():
        pltpu.make_async_copy(last_out, last_all.at[mine, me], last_recv.at[0]).start()

    @pl.when(own != LAST)
    def _():
        send_last().start()

    def rows_of(index):
        return pl.ds(pl.multiple_of(index * 16, 16), 16)

    def send_recv(freq, step):
        peer = ahead(step)
        return remote(
            recv.at[owned(peer) * SPAN + freq], points.at[freq, :, rows_of(me), :],
            recv_send.at[freq], recv_recv.at[freq], shot=peer,
        )

    def own_recv(source, freq):
        return pltpu.make_async_copy(
            recv.at[source], points.at[freq, :, rows_of(me), :], recv_recv.at[freq]
        )

    def send_recv_last():
        return remote(
            recv.at[SHOTS * SPAN], points.at[SPAN, :, rows_of(me), :],
            recv_send.at[SPAN], recv_recv.at[SPAN], shot=last_home,
        )

    @pl.when(own == LAST)
    def _():
        own_recv(SHOTS * SPAN, SPAN).start()

    @pl.when(own != LAST)
    def _():
        send_recv_last().start()

    @pl.loop(0, SPAN)
    def _(freq):
        own_recv(own * SPAN + freq, freq).start()

        @pl.loop(1, SHOTS)
        def _(step):
            send_recv(freq, step).start()

    def arrived(buffer, index, sem):
        whole = buffer.at[index]
        pltpu.make_async_copy(whole, whole, sem).wait()

    def gather(kind, buffer, step):
        return remote(
            buffer.at[mine], buffer.at[mine], gather_send.at[kind, step], gather_recv.at[kind, step],
            **beside(step),
        )

    arrived(spec_all, mine, spec_recv.at[0])
    arrived(meta_all, mine, meta_recv.at[0])

    @pl.when(own == LAST)
    def _():
        arrived(last_all, mine, last_recv.at[0])

    @pl.loop(1, PARTS)
    def _(step):
        gather(0, spec_all, step).start()
        gather(1, meta_all, step).start()

        @pl.when(own == LAST)
        def _():
            gather(2, last_all, step).start()

    def place_rows(index):
        meta = jnp.concatenate([meta_all[index, source] for source in range(SHOTS)], axis=1)
        values = jnp.concatenate([spec_all[index, source] for source in range(SHOTS)], axis=1)
        final_values = jnp.concatenate([last_all[index, source] for source in range(SHOTS)], axis=1)
        values, final_values = values.astype(F32), final_values.astype(F32)
        owner = meta // (256 * 4096)
        place = meta // 4096 % 256
        shot = (meta // 256 % 16 + 1).astype(F32)
        point = (meta % 256).astype(F32)
        hit = owner == lax.broadcasted_iota(jnp.int32, (SHOTS, 2048), 0)
        lines = [jnp.where(owner == block, values, 0.0).astype(BF16) for block in range(SHOTS)]
        for line in (final_values[0:1], final_values[1:2], shot, point):
            lines.append(jnp.where(hit, line, 0.0).astype(BF16))
        target = (place == lax.broadcasted_iota(jnp.int32, (256, 2048), 0)).astype(F32).astype(BF16)
        routed = lax.dot_general(
            jnp.concatenate(lines, axis=0), target, NT, preferred_element_type=F32
        )
        places = pl.ds(pl.multiple_of(index * 256, 256), 256)
        slots[:, :, places] = routed[:256].reshape(SHOTS, 16, 256)
        extras[:, :, places] = routed[256:].reshape(4, SHOTS, 256)

    place_rows(mine)

    @pl.loop(1, PARTS)
    def _(step):
        index = beside_back(step)
        arrived(spec_all, index, gather_recv.at[0, step])
        arrived(meta_all, index, gather_recv.at[1, step])

        @pl.when(own == LAST)
        def _():
            arrived(last_all, index, gather_recv.at[2, step])

        place_rows(index)

    @pl.loop(0, SHOTS, unroll=8)
    def _(block):
        line_of = pl.ds(block, 1)
        shot_hit = extras[2, line_of, :] == (
            lax.broadcasted_iota(jnp.int32, (16, 2048), 0) + 1
        ).astype(F32)
        lines = [
            jnp.where(shot_hit, slots[block, line : line + 1, :], 0.0).astype(BF16)
            for line in range(16)
        ]
        lines += [jnp.where(shot_hit, extras[line, line_of, :], 0.0).astype(BF16) for line in (0, 1)]
        lines.append(shot_hit.astype(F32).astype(BF16))
        point_hit = (
            extras[3, line_of, :] == lax.broadcasted_iota(jnp.int32, (POINTS, 2048), 0).astype(F32)
        ).astype(F32).astype(BF16)
        sums = lax.dot_general(
            jnp.concatenate(lines, axis=0), point_hit, NT, preferred_element_type=F32
        )
        scale = 1.0 / jnp.maximum(sums[288:304], 1.0)
        panel[:, rows_of(block), :] = (
            sums[:288].reshape(18, 16, POINTS) * scale[None]
        ).astype(BF16)

    def swap(freq):
        return remote(
            part.at[freq, 1 - core], other.at[freq], swap_send.at[freq], swap_recv.at[freq],
            surf=1 - core,
        )

    def multiply(freq):
        pltpu.make_async_copy(points.at[freq], points.at[freq], recv_recv.at[freq]).wait()
        both = jnp.concatenate([points[freq, 0], points[freq, 1]], axis=1)
        shots = panel[pl.ds(2 * freq, 2)].reshape(512, POINTS)
        terms = jnp.dot(shots, both, preferred_element_type=F32)
        real = terms[:256, :RCV] - terms[256:, RCV:]
        imag = terms[:256, RCV:] + terms[256:, :RCV]
        for index, value in enumerate((real, imag)):
            split = value.reshape(SHOTS, 2, 8, RCV)
            for half in range(2):
                part[freq, half, index] = split[:, half].astype(BF16)
        swap(freq).start()

    def send_out(freq, step):
        peer = ahead(step)
        return remote(
            final.at[freq, :, peer], out.at[own * SPAN + freq], out_send.at[freq], out_recv.at[0],
            shot=peer,
        )

    def send_out_last(step):
        peer = ahead(step)
        return remote(
            final.at[SPAN, :, peer], out.at[SHOTS * SPAN], out_send.at[SPAN], out_recv.at[0],
            shot=peer,
        )

    def combine(freq):
        swap(freq).wait()
        total = part[freq, core].astype(F32) + other[freq].astype(F32)
        final[freq] = total.astype(BF16)

    def finish(freq):
        combine(freq)
        pltpu.make_async_copy(final.at[freq, :, me], out.at[own * SPAN + freq], out_recv.at[0]).start()

        @pl.loop(1, SHOTS)
        def _(step):
            @pl.when((freq < DEFER) | (ahead(step) % 8 < FIRST))
            def _():
                send_out(freq, step).start()

    @pl.when(own == LAST)
    def _():
        multiply(SPAN)

    multiply(0)

    @pl.when(own == LAST)
    def _():
        combine(SPAN)
        pltpu.make_async_copy(final.at[SPAN, :, me], out.at[SHOTS * SPAN], out_recv.at[0]).start()

        @pl.loop(1, SHOTS)
        def _(step):
            send_out_last(step).start()

    @pl.loop(1, SPAN)
    def _(freq):
        multiply(freq)
        finish(freq - 1)

    finish(SPAN - 1)

    @pl.loop(DEFER, SPAN)
    def _(freq):
        @pl.loop(1, SHOTS)
        def _(step):
            @pl.when(ahead(step) % 8 >= FIRST)
            def _():
                send_out(freq, step).start()

    @pl.loop(1, SHOTS)
    def _(step):
        for copy in send_spec(step):
            copy.wait_send()

    @pl.loop(1, PARTS)
    def _(step):
        gather(0, spec_all, step).wait_send()
        gather(1, meta_all, step).wait_send()

        @pl.when(own == LAST)
        def _():
            gather(2, last_all, step).wait_send()

    @pl.when(own != LAST)
    def _():
        send_last().wait_send()
        send_recv_last().wait_send()

    @pl.loop(0, SPAN)
    def _(freq):
        sent = points.at[freq, :, pl.ds(0, 240), :]
        pltpu.make_async_copy(sent, sent, recv_send.at[freq]).wait()
        sent = final.at[freq, :, pl.ds(0, SHOTS - 1)]
        pltpu.make_async_copy(sent, sent, out_send.at[freq]).wait()

    @pl.when(own == LAST)
    def _():
        sent = final.at[SPAN, :, pl.ds(0, SHOTS - 1)]
        pltpu.make_async_copy(sent, sent, out_send.at[SPAN]).wait()

    pltpu.make_async_copy(out, out, out_recv.at[0]).wait()


def local(traces, trace_block, trace_shot, trace_point, recv_panel):
    rows, window = traces.shape[1:]
    freqs = recv_panel.shape[0]
    high, low = transform_table(window, freqs)
    hbm = pl.BlockSpec(memory_space=pltpu.HBM)
    dma = pltpu.SemaphoreType.DMA
    return pl.pallas_call(
        kernel,
        out_shape=jax.ShapeDtypeStruct((freqs, 2, 8, RCV), BF16),
        in_specs=[hbm] * 7,
        out_specs=pl.BlockSpec(memory_space=pl.ANY),
        scratch_shapes=[
            pltpu.VMEM((PART, window), BF16),
            pltpu.VMEM(high.shape, BF16),
            pltpu.VMEM(low.shape, BF16),
            pltpu.VMEM((3, 1, PART), jnp.int32),
            pltpu.VMEM((SHOTS, 16, PART), BF16),
            pltpu.VMEM((PARTS, SHOTS, 16, PART), BF16),
            pltpu.VMEM((2, PART), BF16),
            pltpu.VMEM((PARTS, SHOTS, 2, PART), BF16),
            pltpu.VMEM((1, PART), jnp.int32),
            pltpu.VMEM((PARTS, SHOTS, 1, PART), jnp.int32),
            pltpu.VMEM((SHOTS, 16, 2048), F32),
            pltpu.VMEM((4, SHOTS, 2048), F32),
            pltpu.VMEM((18, 256, POINTS), BF16),
            pltpu.VMEM((SPAN + 1, 2, POINTS, RCV), BF16),
            pltpu.VMEM((SPAN + 1, 2, 2, SHOTS, 8, RCV), BF16),
            pltpu.VMEM((SPAN + 1, 2, SHOTS, 8, RCV), BF16),
            pltpu.VMEM((SPAN + 1, 2, SHOTS, 8, RCV), BF16),
            dma((6,)), dma((SHOTS,)), dma((1,)), dma((1,)), dma((1,)), dma((SHOTS,)), dma((1,)),
            dma((3, PARTS)), dma((3, PARTS)),
            dma((SPAN + 1,)), dma((SPAN + 1,)), dma((SPAN + 1,)), dma((SPAN + 1,)),
            dma((SPAN + 1,)), dma((1,)),
        ],
        compiler_params=pltpu.CompilerParams(collective_id=0, has_side_effects=True, vmem_limit_bytes=48 * 1024 * 1024),
        name="multiples",
    )(
        *(
            pltpu.with_memory_space_constraint(array, pltpu.HBM)
            for array in (
                traces, trace_block.reshape(1, rows), trace_shot, trace_point,
                jnp.asarray(high), jnp.asarray(low), recv_panel,
            )
        )
    )


def solution(mesh):
    in_specs = (
        P("surf", "shot", None),
        P("surf", "shot", None),
        P("surf", "shot"),
        P("surf", "shot"),
        P(None, None, ("shot", "surf"), "rcv"),
    )
    out_specs = P(None, None, ("shot", "surf"), "rcv")
    return jax.shard_map(local, mesh=mesh, in_specs=in_specs, out_specs=out_specs, check_vma=False)
```

```python
import math

import jax
import jax.numpy as jnp
import numpy as np
from jax import lax
from jax.experimental import pallas as pl
from jax.experimental.pallas import tpu as pltpu
from jax.sharding import PartitionSpec as P

SHOTS = 16
SPAN = 8
PART = 128
PARTS = 8
CAP = 16
FIRST = 3
DEFER = 4
LAST = 15
POINTS = 256
RCV = 128
F32 = jnp.float32
BF16 = jnp.bfloat16
NT = (((1,), (1,)), ((), ()))


def transform_table(window, freqs):
    phase = (np.arange(freqs)[:, None] * np.arange(window)[None, :] % window) * (2 * math.pi / window)
    table = np.zeros((2 * freqs + 6, window), np.float32)
    table[0 : 2 * freqs : 2] = np.cos(phase) / math.sqrt(window)
    table[1 : 2 * freqs : 2] = -np.sin(phase) / math.sqrt(window)
    high = table.astype(BF16)
    return high, (table - high.astype(np.float32)).astype(BF16)


def kernel(
    traces, block_ids, shot_ids, point_ids, table_high, table_low, recv, out,
    samples, high, low, ids, spec_out, spec_all, last_out, last_all, meta_out, meta_all,
    slots, extras, panel, points, part, other, final,
    load_sem, spec_send, spec_recv, last_send, last_recv, meta_send, meta_recv,
    gather_send, gather_recv,
    recv_send, recv_recv, swap_send, swap_recv, out_send, out_recv,
):
    me = lax.axis_index("shot")
    mine = lax.axis_index("rcv")
    row, side = mine // 2, mine % 2
    core = lax.axis_index("surf")
    column, ring = me // 8, me % 8

    def ahead(step):
        return (column + step % 2) % 2 * 8 + (ring + step // 2) % 8

    def owned(index):
        return (index // 8 + side) % 2 * 8 + index % 8

    own = owned(me)
    last_home = owned(LAST)

    def beside(step):
        return {
            "shot": (column + step % 2) % 2 * 8 + ring,
            "rcv": (row + step // 2) % 4 * 2 + (side + step % 2) % 2,
        }

    def beside_back(step):
        return (row + 4 - step // 2) % 4 * 2 + (side + step % 2) % 2

    def remote(src, dst, send, arrive, **where):
        return pltpu.make_async_remote_copy(
            src_ref=src, dst_ref=dst, send_sem=send, recv_sem=arrive,
            device_id=where, device_id_type=pl.DeviceIdType.MESH,
        )

    lanes = pl.ds(pl.multiple_of(mine * PART, PART), PART)
    loads = [
        pltpu.make_async_copy(traces.at[0, lanes, :], samples, load_sem.at[0]),
        pltpu.make_async_copy(table_high, high, load_sem.at[1]),
        pltpu.make_async_copy(table_low, low, load_sem.at[2]),
        pltpu.make_async_copy(block_ids.at[:, lanes], ids.at[0], load_sem.at[3]),
        pltpu.make_async_copy(shot_ids.at[:, lanes], ids.at[1], load_sem.at[4]),
        pltpu.make_async_copy(point_ids.at[:, lanes], ids.at[2], load_sem.at[5]),
    ]
    for load in loads:
        load.start()

    barrier = pltpu.get_barrier_semaphore()

    @pl.loop(1, SHOTS)
    def _(step):
        pl.semaphore_signal(
            barrier, inc=1, device_id={"shot": ahead(step)}, device_id_type=pl.DeviceIdType.MESH
        )

    @pl.loop(1, PARTS)
    def _(step):
        pl.semaphore_signal(
            barrier, inc=1, device_id=beside(step), device_id_type=pl.DeviceIdType.MESH
        )

    pl.semaphore_signal(
        barrier, inc=1, device_id={"surf": 1 - core}, device_id_type=pl.DeviceIdType.MESH
    )

    @pl.when(own != LAST)
    def _():
        last_all[...] = jnp.zeros_like(last_all)

    for load in loads:
        load.wait()

    spectra = lax.dot_general(high[...], samples[...], NT, preferred_element_type=F32)
    spectra += lax.dot_general(low[...], samples[...], NT, preferred_element_type=F32)
    spec_out[...] = spectra[:256].reshape(SHOTS, 16, PART).astype(BF16)
    last_out[...] = spectra[256:258].astype(BF16)

    earlier = (
        lax.broadcasted_iota(jnp.int32, (PART, PART), 0)
        < lax.broadcasted_iota(jnp.int32, (PART, PART), 1)
    ).astype(F32).astype(BF16)
    owners = ids[0]
    hits = owners == lax.broadcasted_iota(jnp.int32, (SHOTS, PART), 0)
    before = jnp.dot(hits.astype(F32).astype(BF16), earlier, preferred_element_type=F32)
    rank = jnp.sum(jnp.where(hits, before, 0.0), axis=0, keepdims=True).astype(jnp.int32)
    meta_out[...] = (owners * 256 + me * CAP + rank) * 4096 + ids[1] * 256 + ids[2]

    pl.semaphore_wait(barrier, SHOTS - 1 + PARTS - 1 + 1)

    def send_spec(step):
        peer = ahead(step)
        return (
            remote(spec_out.at[owned(peer)], spec_all.at[mine, me], spec_send.at[step], spec_recv.at[0], shot=peer),
            remote(meta_out, meta_all.at[mine, me], meta_send.at[step], meta_recv.at[0], shot=peer),
        )

    def send_last():
        return remote(last_out, last_all.at[mine, me], last_send.at[0], last_recv.at[0], shot=last_home)

    @pl.loop(1, SHOTS)
    def _(step):
        for copy in send_spec(step):
            copy.start()

    pltpu.make_async_copy(spec_out.at[own], spec_all.at[mine, me], spec_recv.at[0]).start()
    pltpu.make_async_copy(meta_out, meta_all.at[mine, me], meta_recv.at[0]).start()

    @pl.when(own == LAST)
    def _():
        pltpu.make_async_copy(last_out, last_all.at[mine, me], last_recv.at[0]).start()

    @pl.when(own != LAST)
    def _():
        send_last().start()

    def rows_of(index):
        return pl.ds(pl.multiple_of(index * 16, 16), 16)

    def send_recv(freq, step):
        peer = ahead(step)
        return remote(
            recv.at[owned(peer) * SPAN + freq], points.at[freq, :, rows_of(me), :],
            recv_send.at[freq], recv_recv.at[freq], shot=peer,
        )

    def own_recv(source, freq):
        return pltpu.make_async_copy(
            recv.at[source], points.at[freq, :, rows_of(me), :], recv_recv.at[freq]
        )

    def send_recv_last():
        return remote(
            recv.at[SHOTS * SPAN], points.at[SPAN, :, rows_of(me), :],
            recv_send.at[SPAN], recv_recv.at[SPAN], shot=last_home,
        )

    @pl.when(own == LAST)
    def _():
        own_recv(SHOTS * SPAN, SPAN).start()

    @pl.when(own != LAST)
    def _():
        send_recv_last().start()

    @pl.loop(0, SPAN)
    def _(freq):
        own_recv(own * SPAN + freq, freq).start()

        @pl.loop(1, SHOTS)
        def _(step):
            send_recv(freq, step).start()

    def arrived(buffer, index, sem):
        whole = buffer.at[index]
        pltpu.make_async_copy(whole, whole, sem).wait()

    def gather(kind, buffer, step):
        return remote(
            buffer.at[mine], buffer.at[mine], gather_send.at[kind, step], gather_recv.at[kind, step],
            **beside(step),
        )

    arrived(spec_all, mine, spec_recv.at[0])
    arrived(meta_all, mine, meta_recv.at[0])

    @pl.when(own == LAST)
    def _():
        arrived(last_all, mine, last_recv.at[0])

    @pl.loop(1, PARTS)
    def _(step):
        gather(0, spec_all, step).start()
        gather(1, meta_all, step).start()

        @pl.when(own == LAST)
        def _():
            gather(2, last_all, step).start()

    def place_rows(index):
        meta = jnp.concatenate([meta_all[index, source] for source in range(SHOTS)], axis=1)
        values = jnp.concatenate([spec_all[index, source] for source in range(SHOTS)], axis=1)
        final_values = jnp.concatenate([last_all[index, source] for source in range(SHOTS)], axis=1)
        values, final_values = values.astype(F32), final_values.astype(F32)
        owner = meta // (256 * 4096)
        place = meta // 4096 % 256
        shot = (meta // 256 % 16 + 1).astype(F32)
        point = (meta % 256).astype(F32)
        hit = owner == lax.broadcasted_iota(jnp.int32, (SHOTS, 2048), 0)
        lines = [jnp.where(owner == block, values, 0.0).astype(BF16) for block in range(SHOTS)]
        for line in (final_values[0:1], final_values[1:2], shot, point):
            lines.append(jnp.where(hit, line, 0.0).astype(BF16))
        target = (place == lax.broadcasted_iota(jnp.int32, (256, 2048), 0)).astype(F32).astype(BF16)
        routed = lax.dot_general(
            jnp.concatenate(lines, axis=0), target, NT, preferred_element_type=F32
        )
        places = pl.ds(pl.multiple_of(index * 256, 256), 256)
        slots[:, :, places] = routed[:256].reshape(SHOTS, 16, 256)
        extras[:, :, places] = routed[256:].reshape(4, SHOTS, 256)

    place_rows(mine)

    @pl.loop(1, PARTS)
    def _(step):
        index = beside_back(step)
        arrived(spec_all, index, gather_recv.at[0, step])
        arrived(meta_all, index, gather_recv.at[1, step])

        @pl.when(own == LAST)
        def _():
            arrived(last_all, index, gather_recv.at[2, step])

        place_rows(index)

    @pl.loop(0, SHOTS, unroll=8)
    def _(block):
        line_of = pl.ds(block, 1)
        shot_hit = extras[2, line_of, :] == (
            lax.broadcasted_iota(jnp.int32, (16, 2048), 0) + 1
        ).astype(F32)
        lines = [
            jnp.where(shot_hit, slots[block, line : line + 1, :], 0.0).astype(BF16)
            for line in range(16)
        ]
        lines += [jnp.where(shot_hit, extras[line, line_of, :], 0.0).astype(BF16) for line in (0, 1)]
        lines.append(shot_hit.astype(F32).astype(BF16))
        point_hit = (
            extras[3, line_of, :] == lax.broadcasted_iota(jnp.int32, (POINTS, 2048), 0).astype(F32)
        ).astype(F32).astype(BF16)
        sums = lax.dot_general(
            jnp.concatenate(lines, axis=0), point_hit, NT, preferred_element_type=F32
        )
        scale = 1.0 / jnp.maximum(sums[288:304], 1.0)
        panel[:, rows_of(block), :] = (
            sums[:288].reshape(18, 16, POINTS) * scale[None]
        ).astype(BF16)

    def swap(freq):
        return remote(
            part.at[freq, 1 - core], other.at[freq], swap_send.at[freq], swap_recv.at[freq],
            surf=1 - core,
        )

    def multiply(freq):
        pltpu.make_async_copy(points.at[freq], points.at[freq], recv_recv.at[freq]).wait()
        both = jnp.concatenate([points[freq, 0], points[freq, 1]], axis=1)
        shots = panel[pl.ds(2 * freq, 2)].reshape(512, POINTS)
        terms = jnp.dot(shots, both, preferred_element_type=F32)
        real = terms[:256, :RCV] - terms[256:, RCV:]
        imag = terms[:256, RCV:] + terms[256:, :RCV]
        for index, value in enumerate((real, imag)):
            split = value.reshape(SHOTS, 2, 8, RCV)
            for half in range(2):
                part[freq, half, index] = split[:, half].astype(BF16)
        swap(freq).start()

    def send_out(freq, step):
        peer = ahead(step)
        return remote(
            final.at[freq, :, peer], out.at[own * SPAN + freq], out_send.at[freq], out_recv.at[0],
            shot=peer,
        )

    def send_out_last(step):
        peer = ahead(step)
        return remote(
            final.at[SPAN, :, peer], out.at[SHOTS * SPAN], out_send.at[SPAN], out_recv.at[0],
            shot=peer,
        )

    def combine(freq):
        swap(freq).wait()
        total = part[freq, core].astype(F32) + other[freq].astype(F32)
        final[freq] = total.astype(BF16)

    def finish(freq):
        combine(freq)
        pltpu.make_async_copy(final.at[freq, :, me], out.at[own * SPAN + freq], out_recv.at[0]).start()

        @pl.loop(1, SHOTS)
        def _(step):
            @pl.when((freq < DEFER) | (ahead(step) % 8 < FIRST))
            def _():
                send_out(freq, step).start()

    @pl.when(own == LAST)
    def _():
        multiply(SPAN)

    multiply(0)

    @pl.when(own == LAST)
    def _():
        combine(SPAN)
        pltpu.make_async_copy(final.at[SPAN, :, me], out.at[SHOTS * SPAN], out_recv.at[0]).start()

        @pl.loop(1, SHOTS)
        def _(step):
            send_out_last(step).start()

    @pl.loop(1, SPAN)
    def _(freq):
        multiply(freq)
        finish(freq - 1)

    finish(SPAN - 1)

    @pl.loop(DEFER, SPAN)
    def _(freq):
        @pl.loop(1, SHOTS)
        def _(step):
            @pl.when(ahead(step) % 8 >= FIRST)
            def _():
                send_out(freq, step).start()

    @pl.loop(1, SHOTS)
    def _(step):
        for copy in send_spec(step):
            copy.wait_send()

    @pl.loop(1, PARTS)
    def _(step):
        gather(0, spec_all, step).wait_send()
        gather(1, meta_all, step).wait_send()

        @pl.when(own == LAST)
        def _():
            gather(2, last_all, step).wait_send()

    @pl.when(own != LAST)
    def _():
        send_last().wait_send()
        send_recv_last().wait_send()

    @pl.loop(0, SPAN)
    def _(freq):
        sent = points.at[freq, :, pl.ds(0, 240), :]
        pltpu.make_async_copy(sent, sent, recv_send.at[freq]).wait()
        sent = final.at[freq, :, pl.ds(0, SHOTS - 1)]
        pltpu.make_async_copy(sent, sent, out_send.at[freq]).wait()

    @pl.when(own == LAST)
    def _():
        sent = final.at[SPAN, :, pl.ds(0, SHOTS - 1)]
        pltpu.make_async_copy(sent, sent, out_send.at[SPAN]).wait()

    pltpu.make_async_copy(out, out, out_recv.at[0]).wait()


def local(traces, trace_block, trace_shot, trace_point, recv_panel):
    rows, window = traces.shape[1:]
    freqs = recv_panel.shape[0]
    high, low = transform_table(window, freqs)
    hbm = pl.BlockSpec(memory_space=pltpu.HBM)
    dma = pltpu.SemaphoreType.DMA
    return pl.pallas_call(
        kernel,
        out_shape=jax.ShapeDtypeStruct((freqs, 2, 8, RCV), BF16),
        in_specs=[hbm] * 7,
        out_specs=pl.BlockSpec(memory_space=pl.ANY),
        scratch_shapes=[
            pltpu.VMEM((PART, window), BF16),
            pltpu.VMEM(high.shape, BF16),
            pltpu.VMEM(low.shape, BF16),
            pltpu.VMEM((3, 1, PART), jnp.int32),
            pltpu.VMEM((SHOTS, 16, PART), BF16),
            pltpu.VMEM((PARTS, SHOTS, 16, PART), BF16),
            pltpu.VMEM((2, PART), BF16),
            pltpu.VMEM((PARTS, SHOTS, 2, PART), BF16),
            pltpu.VMEM((1, PART), jnp.int32),
            pltpu.VMEM((PARTS, SHOTS, 1, PART), jnp.int32),
            pltpu.VMEM((SHOTS, 16, 2048), F32),
            pltpu.VMEM((4, SHOTS, 2048), F32),
            pltpu.VMEM((18, 256, POINTS), BF16),
            pltpu.VMEM((SPAN + 1, 2, POINTS, RCV), BF16),
            pltpu.VMEM((SPAN + 1, 2, 2, SHOTS, 8, RCV), BF16),
            pltpu.VMEM((SPAN + 1, 2, SHOTS, 8, RCV), BF16),
            pltpu.VMEM((SPAN + 1, 2, SHOTS, 8, RCV), BF16),
            dma((6,)), dma((SHOTS,)), dma((1,)), dma((1,)), dma((1,)), dma((SHOTS,)), dma((1,)),
            dma((3, PARTS)), dma((3, PARTS)),
            dma((SPAN + 1,)), dma((SPAN + 1,)), dma((SPAN + 1,)), dma((SPAN + 1,)),
            dma((SPAN + 1,)), dma((1,)),
        ],
        compiler_params=pltpu.CompilerParams(collective_id=0, has_side_effects=True, vmem_limit_bytes=48 * 1024 * 1024),
        name="multiples",
    )(
        *(
            pltpu.with_memory_space_constraint(array, pltpu.HBM)
            for array in (
                traces, trace_block.reshape(1, rows), trace_shot, trace_point,
                jnp.asarray(high), jnp.asarray(low), recv_panel,
            )
        )
    )


def solution(mesh):
    in_specs = (
        P("surf", "shot", None),
        P("surf", "shot", None),
        P("surf", "shot"),
        P("surf", "shot"),
        P(None, None, ("shot", "surf"), "rcv"),
    )
    out_specs = P(None, None, ("shot", "surf"), "rcv")
    return jax.shard_map(local, mesh=mesh, in_specs=in_specs, out_specs=out_specs, check_vma=False)
```
